32 devices in a mesh: ctx: 16 (over z, y, x), head: 2 (over core).
Axes of the slice: x: 2, y: 2, z: 4, core: 2. Of those that a mesh axis runs over, the one named last changes fastest.
Arguments:
- queries: bfloat16 [512, 8192], P('ctx', 'head'), may hold values from -6 to 6
- cache_keys: bfloat16 [16384, 8, 128], P('ctx', 'head'), may hold values from -6 to 6
- cache_values: bfloat16 [16384, 8, 128], P('ctx', 'head'), may hold values from -6 to 6
- vertical_blocks: int32 [64, 8], P('head'), may hold values from 0 to 127, as said below
- slash_offsets: int32 [64, 48], P('head'), may hold values from 0 to 127, as said below
- out_weight: bfloat16 [8192, 8192], P('head', 'ctx'), may hold values from -0.0625 to 0.0625
Outputs:
- projected: bfloat16 [512, 8192], P('head', 'ctx')
The draws below stay inside these ranges and needn't reach their ends.
Inputs may be any that keep to these rules, and one draw needn't show every extreme that they name: `vertical_blocks`: every head's list holds block 0; entries may repeat, and a block counts once however often it is named. `slash_offsets`: every head's list holds offset 0; entries may repeat, and a block counts once however often it is reached.
All inputs are finite; a program needn't handle non-finite values.
Results may differ from the reference program's by a relative error of at most 0.007.
Values may be sent and summed in bfloat16 or wider, within the bound.
No kernel may reach another device: no remote copies, remote signals or barrier semaphores. Data moves between devices by JAX's collectives and lax.ppermute only.
A program may use at most 128 MiB of HBM per device.

```python
from functools import partial
import jax
import jax.numpy as jnp
from jax import lax

D = 8192
HEADS = 64
KV_HEADS = 8
HEAD_DIM = 128
BLOCK = 128
NV = 8
NS = 48
Q_LEN = 512
CTX_DEV = 1024
GROUP = 8
CONTEXT = 16384
KB_ALL = 128
Q_BLOCKS = 4


def draw_queries(key, part):
    noise_key = jax.random.fold_in(key, 1)
    shape_four = (Q_LEN, KV_HEADS, GROUP, HEAD_DIM)
    drawn = jnp.clip(jax.random.normal(noise_key, shape_four, dtype=jnp.float32), -4.0, 4.0)
    return drawn.reshape(Q_LEN, HEADS * HEAD_DIM).astype(jnp.bfloat16)


def draw_cache_keys(key, part):
    noise_key = jax.random.fold_in(key, 2)
    shape_three = (CONTEXT, KV_HEADS, HEAD_DIM)
    drawn = jnp.clip(jax.random.normal(noise_key, shape_three, dtype=jnp.float32), -4.0, 4.0)
    return drawn.astype(jnp.bfloat16)


def draw_vertical_blocks(key, part):
    picks = jax.random.randint(jax.random.fold_in(key, 11), (HEADS, NV), 1, KB_ALL)
    which = jax.random.randint(jax.random.fold_in(key, 12), (), 0, HEADS)
    picks = picks.at[:, 0].set(0)
    picks = picks.at[:, 1].set(jnp.where(jnp.arange(HEADS) == which, KB_ALL - 1, picks[:, 1]))
    return picks.astype(jnp.int32)


def draw_slash_offsets(key, part):
    near = jax.random.randint(jax.random.fold_in(key, 13), (HEADS, NS), 0, 2 * CTX_DEV // BLOCK)
    far = jax.random.randint(jax.random.fold_in(key, 14), (HEADS, NS), 0, KB_ALL)
    coin = jax.random.randint(jax.random.fold_in(key, 15), (HEADS, NS), 0, 4)
    picks = jnp.where(coin == 0, far, near)
    which = jax.random.randint(jax.random.fold_in(key, 16), (), 0, HEADS)
    picks = picks.at[:, 0].set(0)
    picks = picks.at[:, 1].set(jnp.where(jnp.arange(HEADS) == which, KB_ALL - 1, picks[:, 1]))
    return picks.astype(jnp.int32)


def shard_levels(rng, extent, shards, smallest, high):
    loudness, own = 1.0, jax.random.fold_in(rng, 6)
    for dim, blocks in shards:
        steps = jnp.exp(jax.random.uniform(jax.random.fold_in(own, dim), (blocks,), jnp.float32, smallest / len(shards), high / len(shards)))
        loudness = loudness * jnp.repeat(steps, extent[dim] // blocks).reshape([-1 if axis == dim else 1 for axis in range(len(extent))])
    return loudness


def gaussian(key, shape, spread, bound, pieces=(), kind=jnp.bfloat16):
    gain = shard_levels(key, shape, pieces, -0.22, 0.18) if pieces else 1.0
    result = jax.random.normal(key, shape, jnp.float32) * spread * gain
    return jnp.minimum(jnp.maximum(result, -bound), bound).astype(kind)


def setup_inputs(seed: int = 0) -> dict:
    seeds = jax.random.split(jax.random.key(seed), 7)
    return {
        "queries": draw_queries(jax.random.fold_in(seeds[6], 71), 0),
        "cache_keys": draw_cache_keys(jax.random.fold_in(seeds[6], 71), 0),
        "cache_values": gaussian(seeds[2], (CONTEXT, KV_HEADS, HEAD_DIM), 1.0, 6.0, ((0, 16), (1, 2))),
        "vertical_blocks": draw_vertical_blocks(jax.random.fold_in(seeds[6], 71), 0),
        "slash_offsets": draw_slash_offsets(jax.random.fold_in(seeds[6], 71), 0),
        "out_weight": gaussian(seeds[5], (HEADS * HEAD_DIM, D), (HEADS * HEAD_DIM) ** -0.5, 0.0625, ((0, 2), (1, 16))),
    }


NEG_FILL = -1e30


def head_rows(head_index, queries, cache_keys, cache_values, vertical_blocks, slash_offsets):
    group_index = head_index // GROUP
    key_rows = lax.dynamic_index_in_dim(cache_keys, group_index, 1, keepdims=False).reshape(KB_ALL, BLOCK, HEAD_DIM)
    value_rows = lax.dynamic_index_in_dim(cache_values, group_index, 1, keepdims=False).reshape(KB_ALL, BLOCK, HEAD_DIM)
    query_rows = lax.dynamic_index_in_dim(queries.reshape(Q_LEN, HEADS, HEAD_DIM), head_index, 1, keepdims=False)
    vertical_row = lax.dynamic_index_in_dim(vertical_blocks, head_index, 0, keepdims=False)
    slash_row = lax.dynamic_index_in_dim(slash_offsets, head_index, 0, keepdims=False)
    position = jnp.arange(NV + NS, dtype=jnp.int32)

    def query_block(block_index):
        global_block = KB_ALL - Q_BLOCKS + block_index
        candidates = jnp.concatenate([vertical_row.astype(jnp.int32), (global_block - slash_row).astype(jnp.int32)])
        earlier = (candidates[:, None] == candidates[None, :]) & (position[None, :] < position[:, None])
        usable = (candidates >= 0) & jnp.logical_not(jnp.any(earlier, axis=1))
        clipped = jnp.clip(candidates, 0, KB_ALL - 1).astype(jnp.int32)
        key_tiles = key_rows[clipped].astype(jnp.float32)
        value_tiles = value_rows[clipped].astype(jnp.float32)
        query_tile = lax.dynamic_slice_in_dim(query_rows, (block_index * BLOCK).astype(jnp.int32), BLOCK, 0).astype(jnp.float32)
        scores = jnp.einsum("qd,ckd->qck", query_tile, key_tiles, precision=lax.Precision.HIGHEST) * (HEAD_DIM ** -0.5)
        key_pos = clipped[:, None] * BLOCK + jnp.arange(BLOCK, dtype=jnp.int32)[None, :]
        query_pos = CONTEXT - Q_LEN + block_index * BLOCK + jnp.arange(BLOCK, dtype=jnp.int32)
        allowed_mask = usable[None, :, None] & (key_pos[None, :, :] <= query_pos[:, None, None])
        masked = jnp.where(allowed_mask, scores, NEG_FILL)
        block_peak = jnp.max(masked, axis=-1)
        safe_peak = jnp.where(block_peak > 0.5 * NEG_FILL, block_peak, 0.0)
        weights = jnp.where(allowed_mask, jnp.exp(scores - safe_peak[..., None]), 0.0).astype(jnp.bfloat16)
        weights_wide = weights.astype(jnp.float32)
        block_total = jnp.sum(weights_wide, axis=-1)
        block_out = jnp.einsum("qck,ckd->qcd", weights_wide, value_tiles, precision=lax.Precision.HIGHEST)
        row_peak = jnp.max(block_peak, axis=1)
        factor = jnp.exp(block_peak - row_peak[:, None])
        numer = jnp.sum(factor[..., None] * block_out, axis=1)
        denom = jnp.sum(factor * block_total, axis=1)
        return numer / denom[:, None]

    tiles = lax.map(query_block, jnp.arange(Q_BLOCKS, dtype=jnp.int32))
    return tiles.reshape(Q_LEN, HEAD_DIM)


def reference(queries, cache_keys, cache_values, vertical_blocks, slash_offsets, out_weight):
    one_head = partial(head_rows, queries=queries, cache_keys=cache_keys, cache_values=cache_values,
                       vertical_blocks=vertical_blocks, slash_offsets=slash_offsets)
    per_head = lax.map(one_head, jnp.arange(HEADS, dtype=jnp.int32))
    attention = jnp.transpose(per_head, (1, 0, 2)).reshape(Q_LEN, HEADS * HEAD_DIM).astype(jnp.bfloat16)
    return jnp.dot(attention, out_weight, preferred_element_type=jnp.float32).astype(jnp.bfloat16)
```

```python
from functools import partial
import math

import jax
import jax.numpy as jnp
from jax import lax
from jax.experimental import pallas as pl
from jax.experimental.pallas import tpu as pltpu
from jax.sharding import PartitionSpec as P

BLOCK = 128
NEG_FILL = -1e30
CHUNK = 4
PAIR = 2
ONES_ROWS = 16


def transpose_values_kernel(v_ref, vt_ref):
    blocks = vt_ref.shape[0] - 1
    width = v_ref.shape[1]
    rows = vt_ref.shape[1]
    for i in range(blocks):
        vt_ref[i, 0:width, :] = v_ref[i * BLOCK : (i + 1) * BLOCK, :].T
        vt_ref[i, width:rows, :] = jnp.ones((rows - width, BLOCK), vt_ref.dtype)
    vt_ref[blocks] = jnp.zeros((rows, BLOCK), vt_ref.dtype)


def transpose_values(values):
    keys, width = values.shape
    return pl.pallas_call(
        transpose_values_kernel,
        out_shape=jax.ShapeDtypeStruct((keys // BLOCK + 1, width + ONES_ROWS, BLOCK), values.dtype),
        name="transpose_values",
    )(values)


def attention_kernel(
    turn_ref, count_ref, diag_ref, klist_ref, vlist_ref, q_ref, k_ref, vt_ref, o_ref, lse_ref, m_sc, acc_sc,
    *, scale2, list_len,
):
    heads = o_ref.shape[0]
    width = o_ref.shape[1]
    turn = turn_ref[0]
    diag = diag_ref[turn]

    def scores_of(keys, h):
        q = q_ref[:, h * width : (h + 1) * width]
        return lax.dot_general(keys, q, (((1,), (1,)), ((), ())), preferred_element_type=jnp.float32)

    m_sc[...] = jnp.full(m_sc.shape, NEG_FILL, jnp.float32)
    acc_sc[...] = jnp.zeros(acc_sc.shape, jnp.float32)

    @pl.when(diag >= 0)
    def _():
        keys = k_ref[pl.ds(pl.multiple_of(diag * BLOCK, BLOCK), BLOCK), :]
        values = vt_ref[diag]
        causal = lax.broadcasted_iota(jnp.int32, (BLOCK, BLOCK), 0) <= lax.broadcasted_iota(
            jnp.int32, (BLOCK, BLOCK), 1
        )
        for h in range(heads):
            s = jnp.where(causal, scores_of(keys, h) * scale2, NEG_FILL)
            m = jnp.max(s, axis=0, keepdims=True)
            p = jnp.exp2(s - m).astype(jnp.bfloat16)
            m_sc[h : h + 1, :] = m
            acc_sc[h] = jnp.dot(values, p, preferred_element_type=jnp.float32)

    for h0 in range(0, heads, PAIR):
        group = range(h0, min(h0 + PAIR, heads))
        counts = [count_ref[turn * heads + h] for h in group]
        most = counts[0]
        for c in counts[1:]:
            most = jnp.maximum(most, c)

        def visit(t, carry, group=group, counts=counts):
            out = []
            for i, h in enumerate(group):
                m, acc = carry[i]
                base = (turn * heads + h) * list_len + t * CHUNK
                keys = jnp.concatenate(
                    [
                        k_ref[pl.ds(pl.multiple_of(klist_ref[base + u] * BLOCK, BLOCK), BLOCK), :]
                        for u in range(CHUNK)
                    ],
                    axis=0,
                )
                values = jnp.concatenate([vt_ref[vlist_ref[base + u]] for u in range(CHUNK)], axis=1)
                s = scores_of(keys, h)
                top = jnp.max(s, axis=0, keepdims=True) * scale2
                m_new = jnp.maximum(m, jnp.where(t * CHUNK < counts[i], top, NEG_FILL))
                p = jnp.exp2(s * scale2 - jnp.maximum(m_new, top)).astype(jnp.bfloat16)
                acc = acc * jnp.exp2(m - m_new) + jnp.dot(values, p, preferred_element_type=jnp.float32)
                out.append((m_new, acc))
            return tuple(out)

        start = tuple((m_sc[h : h + 1, :], acc_sc[h]) for h in group)
        done = lax.fori_loop(0, (most + CHUNK - 1) // CHUNK, visit, start)
        for i, h in enumerate(group):
            m, acc = done[i]
            total = acc[width : width + 1, :]
            seen = total > 0.0
            safe = jnp.where(seen, total, 1.0)
            o_ref[h] = (acc[0:width, :] / safe).astype(o_ref.dtype)
            lse_ref[h : h + 1, :] = jnp.where(seen, m + jnp.log2(safe), NEG_FILL)


def block_attention(turn, meta, q, keys, vt):
    count, diag, klist, vlist = meta
    turns = diag.shape[0]
    heads = count.shape[0] // turns
    width = keys.shape[1]
    smem = pl.BlockSpec(memory_space=pltpu.SMEM)
    vmem = pl.BlockSpec(memory_space=pltpu.VMEM)
    return pl.pallas_call(
        partial(
            attention_kernel,
            scale2=float(width) ** -0.5 * math.log2(math.e),
            list_len=klist.shape[0] // count.shape[0],
        ),
        out_shape=(
            jax.ShapeDtypeStruct((heads, width, BLOCK), jnp.bfloat16),
            jax.ShapeDtypeStruct((heads, BLOCK), jnp.float32),
        ),
        in_specs=[smem] * 5 + [vmem] * 3,
        out_specs=(vmem, vmem),
        scratch_shapes=[
            pltpu.VMEM((heads, BLOCK), jnp.float32),
            pltpu.VMEM((heads, width + ONES_ROWS, BLOCK), jnp.float32),
        ],
        name="block_attention",
    )(jnp.full((1,), turn, jnp.int32), count, diag, klist, vlist, q, keys, vt)


def combine_kernel(*refs):
    parts = (len(refs) - 1) // 2
    outs, lses, att_ref = refs[:parts], refs[parts : 2 * parts], refs[-1]
    heads, width = outs[0].shape[0], outs[0].shape[1]
    lse = [ref[...] for ref in lses]
    top = lse[0]
    for x in lse[1:]:
        top = jnp.maximum(top, x)
    weight = [jnp.exp2(x - top) for x in lse]
    total = weight[0]
    for x in weight[1:]:
        total = total + x
    inverse = 1.0 / total
    weight = [x * inverse for x in weight]
    for h in range(heads):
        mixed = outs[0][h].astype(jnp.float32) * weight[0][h : h + 1, :]
        for ref, x in zip(outs[1:], weight[1:]):
            mixed = mixed + ref[h].astype(jnp.float32) * x[h : h + 1, :]
        att_ref[:, h * width : (h + 1) * width] = mixed.T.astype(att_ref.dtype)


def combine(outs, lses):
    heads, width, rows = outs[0].shape
    return pl.pallas_call(
        combine_kernel,
        out_shape=jax.ShapeDtypeStruct((rows, heads * width), jnp.bfloat16),
        name="combine",
    )(*outs, *lses)


def block_lists(vertical, slash, query_blocks, first_block, local_blocks):
    ids = first_block + jnp.arange(local_blocks, dtype=jnp.int32)
    offsets = query_blocks[:, None] - ids[None, :]
    vertical_hit = jnp.any(vertical[:, :, None] == ids[None, None, :], axis=1)
    slash_hit = jnp.any(slash[None, :, :, None] == offsets[:, None, None, :], axis=2)
    picked = (vertical_hit[None] | slash_hit) & (offsets > 0)[:, None, :]
    picked = picked.astype(jnp.int32)
    order = jnp.arange(local_blocks, dtype=jnp.int32)
    rank = jnp.sum(picked[:, :, None, :] * (order[None, :] < order[:, None]), axis=3)
    count = jnp.sum(picked, axis=2)
    list_len = -(-local_blocks // CHUNK) * CHUNK
    slot = jnp.arange(list_len, dtype=jnp.int32)
    wanted = jnp.where(slot[None, None, :] < count[:, :, None], slot[None, None, :], 0)
    match = picked[:, :, None, :] * (rank[:, :, None, :] == wanted[:, :, :, None])
    klist = jnp.sum(match * order, axis=3)
    vlist = jnp.where(slot[None, None, :] < count[:, :, None], klist, local_blocks)
    diag = query_blocks - first_block
    diag = jnp.where((diag >= 0) & (diag < local_blocks), diag, -1)
    return count.reshape(-1), diag, klist.reshape(-1), vlist.reshape(-1)


def plane_body(queries, cache_keys, cache_values, vertical_blocks, slash_offsets, out_weight):
    ctx_count = lax.axis_size("ctx")
    core_count = lax.axis_size("head")
    place = lax.axis_index("ctx")
    local_len, plane, width = cache_keys.shape
    lines = ctx_count // plane
    line, mine = place // plane, place % plane
    q_rows = queries.shape[0]
    heads = vertical_blocks.shape[0] // plane
    feats = heads * width
    columns = out_weight.shape[1]
    span = plane * local_len
    local_blocks = span // BLOCK
    all_blocks = local_blocks * lines
    planes = [[a * plane + b for b in range(plane)] for a in range(lines)]
    swap = partial(
        lax.all_to_all, axis_name="ctx", split_axis=0, concat_axis=0, axis_index_groups=planes, tiled=True
    )

    def along(x, step):
        pairs = [
            (a * plane + b, ((a + step) % lines) * plane + b) for a in range(lines) for b in range(plane)
        ]
        return lax.ppermute(x, "ctx", pairs)

    q_own = swap(jnp.transpose(queries.reshape(q_rows, plane, feats), (1, 0, 2))).reshape(plane * q_rows, feats)
    q_parts = [q_own] + [along(q_own, -k) for k in range(1, lines)]
    keys = swap(jnp.transpose(cache_keys, (1, 0, 2))).reshape(span, width)
    values = swap(jnp.transpose(cache_values, (1, 0, 2))).reshape(span, width)
    keys, values, weight = lax.optimization_barrier((keys, values, out_weight))
    weight = swap(weight.reshape(plane, feats, columns))
    vt = transpose_values(values)

    turns = (line + jnp.arange(lines, dtype=jnp.int32)) % lines
    meta = block_lists(
        lax.dynamic_slice_in_dim(vertical_blocks, mine * heads, heads, 0),
        lax.dynamic_slice_in_dim(slash_offsets, mine * heads, heads, 0),
        all_blocks - lines + turns,
        line * local_blocks,
        local_blocks,
    )
    outs, lses = [None] * lines, [None] * lines
    for k in list(range(1, lines)) + [0]:
        o, l = block_attention(k, meta, q_parts[k], keys, vt)
        outs[k], lses[k] = (along(o, k), along(l, k)) if k else (o, l)
    att = combine(outs, lses)
    full = jnp.zeros((lines, BLOCK, feats), jnp.bfloat16)
    for k in range(lines):
        part = along(att, -k) if k else att
        full = lax.dynamic_update_slice_in_dim(full, part[None], turns[k], 0)

    core = lax.axis_index("head")
    full = full.reshape(core_count, lines * BLOCK // core_count, feats)
    rows = full.shape[1]

    def project(which):
        part = lax.dynamic_index_in_dim(full, which, 0, keepdims=False)
        return jnp.stack(
            [jnp.dot(part, weight[j], preferred_element_type=jnp.float32) for j in range(plane)]
        )

    sums = None
    for step in range(1, core_count):
        away = project((core + step) % core_count).astype(jnp.bfloat16)
        got = lax.ppermute(away, "head", [(a, (a + step) % core_count) for a in range(core_count)])
        got = got.astype(jnp.float32)
        sums = got if sums is None else sums + got
    own = project(core)
    sums = own if sums is None else sums + own
    got = swap(sums.astype(jnp.bfloat16))
    return jnp.sum(got.astype(jnp.float32), axis=0).astype(jnp.bfloat16)


def general_body(queries, cache_keys, cache_values, vertical_blocks, slash_offsets, out_weight):
    ctx_count = lax.axis_size("ctx")
    place = lax.axis_index("ctx")
    local_len, kv_local, width = cache_keys.shape
    heads = vertical_blocks.shape[0] // kv_local
    feats = heads * width
    q_whole = lax.all_gather(queries, "ctx", axis=0, tiled=True)
    q_blocks = q_whole.shape[0] // BLOCK
    local_blocks = local_len // BLOCK
    query_blocks = local_blocks * ctx_count - q_blocks + jnp.arange(q_blocks, dtype=jnp.int32)
    attention = []
    for g in range(kv_local):
        meta = block_lists(
            vertical_blocks[g * heads : (g + 1) * heads],
            slash_offsets[g * heads : (g + 1) * heads],
            query_blocks,
            place * local_blocks,
            local_blocks,
        )
        vt = transpose_values(cache_values[:, g, :])
        outs, lses = [], []
        for b in range(q_blocks):
            q = q_whole[b * BLOCK : (b + 1) * BLOCK, g * feats : (g + 1) * feats]
            o, l = block_attention(b, meta, q, cache_keys[:, g, :], vt)
            outs.append(o)
            lses.append(l)
        out, lse = jnp.stack(outs), jnp.stack(lses)
        factor = jnp.exp2(lse - lax.pmax(lse, "ctx"))
        out, total = lax.psum((out.astype(jnp.float32) * factor[:, :, None, :], factor), "ctx")
        out = (out / total[:, :, None, :]).astype(jnp.bfloat16)
        attention.append(jnp.transpose(out, (0, 3, 1, 2)).reshape(q_blocks * BLOCK, feats))
    return lax.psum_scatter(
        jnp.dot(jnp.concatenate(attention, axis=1), out_weight, preferred_element_type=jnp.float32),
        "head",
        scatter_dimension=0,
        tiled=True,
    ).astype(jnp.bfloat16)


def body(queries, cache_keys, cache_values, vertical_blocks, slash_offsets, out_weight):
    ctx_count = lax.axis_size("ctx")
    lines = queries.shape[0] * ctx_count // BLOCK
    fits = cache_keys.shape[1] * lines == ctx_count and lines % lax.axis_size("head") == 0
    chosen = plane_body if fits else general_body
    return chosen(queries, cache_keys, cache_values, vertical_blocks, slash_offsets, out_weight)


def solution(mesh):
    return jax.shard_map(
        body,
        mesh=mesh,
        in_specs=(
            P("ctx", "head"),
            P("ctx", "head", None),
            P("ctx", "head", None),
            P("head", None),
            P("head", None),
            P("head", "ctx"),
        ),
        out_specs=P("head", "ctx"),
        check_vma=False,
    )
```

```python
from functools import partial
import math

import jax
import jax.numpy as jnp
from jax import lax
from jax.experimental import pallas as pl
from jax.experimental.pallas import tpu as pltpu
from jax.sharding import PartitionSpec as P


BLOCK = 128
NEG_FILL = -1e30
CHUNK = 8
STEP = 2
VMEM_LIMIT = 20 << 20


def attention_kernel(
    turn_ref, count_ref, diag_ref, klist_ref, slist_ref, table_ref, k_ref, v_ref, *refs, scale2, list_len, pieces,
):
    *q_refs, o_ref, q_ref, even_sc, odd_sc, diag_sc = refs
    width = k_ref.shape[1]
    heads = q_ref.shape[1] // width
    turn = turn_ref[0]
    piece_rows = BLOCK // pieces
    for i in range(pieces):
        place = table_ref[turn * pieces + i]
        for j, ref in enumerate(q_refs):

            @pl.when(place // pieces == j)
            def _(i=i, j=j, ref=ref, place=place):
                start = pl.multiple_of((place - j * pieces) * piece_rows, piece_rows)
                q_ref[i * piece_rows : (i + 1) * piece_rows, :] = ref[pl.ds(start, piece_rows), :]

    diag = diag_ref[turn]
    bufs = (even_sc, odd_sc)

    def block_of(ref, index):
        return ref[pl.ds(pl.multiple_of(index * BLOCK, BLOCK), BLOCK), :]

    def scores_of(keys, h):
        q = q_ref[:, h * width : (h + 1) * width]
        s = lax.dot_general(q, keys, (((1,), (1,)), ((), ())), preferred_element_type=jnp.float32)
        return s * scale2

    for buf in bufs:
        buf[list_len] = jnp.full((BLOCK, BLOCK), NEG_FILL, jnp.float32)

    @pl.when(diag >= 0)
    def _():
        keys = block_of(k_ref, diag)
        causal = lax.broadcasted_iota(jnp.int32, (BLOCK, BLOCK), 1) <= lax.broadcasted_iota(
            jnp.int32, (BLOCK, BLOCK), 0
        )
        for h in range(heads):
            diag_sc[h] = jnp.where(causal, scores_of(keys, h), NEG_FILL)

    @pl.when(diag < 0)
    def _():
        diag_sc[...] = jnp.full(diag_sc.shape, NEG_FILL, jnp.float32)

    diag_values = block_of(v_ref, jnp.maximum(diag, 0))
    counts = [count_ref[turn * heads + h] for h in range(heads)]
    chunks = [(c + CHUNK - 1) // CHUNK for c in counts]

    def score_part(h, t, u, top):
        base = (turn * heads + h) * list_len + t * CHUNK + u
        keys = jnp.concatenate([block_of(k_ref, klist_ref[base + i]) for i in range(STEP)], axis=0)
        s = scores_of(keys, h)
        for i in range(STEP):
            part = s[:, i * BLOCK : (i + 1) * BLOCK]
            bufs[h % 2][t * CHUNK + u + i] = part
            top = jnp.maximum(top, part)
        return top

    def value_part(h, t, u, m, total, acc):
        base = (turn * heads + h) * list_len + t * CHUNK + u
        values = jnp.concatenate([block_of(v_ref, klist_ref[base + i]) for i in range(STEP)], axis=0)
        parts = [jnp.exp2(bufs[h % 2][slist_ref[base + i]] - m) for i in range(STEP)]
        for p in parts:
            total = total + p
        p = jnp.concatenate([p.astype(jnp.bfloat16) for p in parts], axis=1)
        return total, acc + jnp.dot(p, values, preferred_element_type=jnp.float32)

    top_start = jnp.full((BLOCK, BLOCK), NEG_FILL, jnp.float32)

    def first(t, top):
        for u in range(0, CHUNK, STEP):
            top = score_part(0, t, u, top)
        return top

    top = lax.fori_loop(0, chunks[0], first, top_start)
    lane = lax.broadcasted_iota(jnp.int32, (BLOCK, BLOCK), 1)
    lse = jnp.full((BLOCK, BLOCK), NEG_FILL, jnp.float32)
    for h in range(heads):
        top = jnp.maximum(jnp.where(counts[h] > 0, top, NEG_FILL), diag_sc[h])
        m = jnp.max(top, axis=1, keepdims=True)
        total = jnp.exp2(diag_sc[h] - m)
        total = jnp.where(diag >= 0, total, 0.0)
        acc = jnp.dot(total.astype(jnp.bfloat16), diag_values, preferred_element_type=jnp.float32)
        if h + 1 < heads:

            def both(t, carry, h=h, m=m):
                top, total, acc = carry
                for u in range(0, CHUNK, STEP):
                    top = score_part(h + 1, t, u, top)
                    total, acc = value_part(h, t, u, m, total, acc)
                return top, total, acc

            top, total, acc = lax.fori_loop(
                0, jnp.maximum(chunks[h], chunks[h + 1]), both, (top_start, total, acc)
            )
        else:

            def last(t, carry, h=h, m=m):
                for u in range(0, CHUNK, STEP):
                    carry = value_part(h, t, u, m, *carry)
                return carry

            total, acc = lax.fori_loop(0, chunks[h], last, (total, acc))
        total = jnp.sum(total, axis=1, keepdims=True)
        seen = total > 0.0
        safe = jnp.where(seen, total, 1.0)
        o_ref[:, h * width : (h + 1) * width] = (acc / safe).astype(o_ref.dtype)
        mine = (lane == h) | (lane == heads + h) | (lane == 2 * heads + h)
        lse = jnp.where(mine & seen, m + jnp.log2(safe), lse)
    high = lse.astype(jnp.bfloat16)
    rest = lse - high.astype(jnp.float32)
    middle = rest.astype(jnp.bfloat16)
    low = rest - middle.astype(jnp.float32)
    packed = jnp.where(lane < heads, high.astype(jnp.float32), jnp.where(lane < 2 * heads, middle.astype(jnp.float32), low))
    o_ref[:, heads * width :] = packed.astype(o_ref.dtype)


def block_attention(turn, meta, table, q_parts, keys, values):
    count, diag, klist, slist = meta
    turns = diag.shape[0]
    heads = count.shape[0] // turns
    width = keys.shape[1]
    list_len = klist.shape[0] // count.shape[0]
    smem = pl.BlockSpec(memory_space=pltpu.SMEM)
    vmem = pl.BlockSpec(memory_space=pltpu.VMEM)
    return pl.pallas_call(
        partial(
            attention_kernel,
            scale2=float(width) ** -0.5 * math.log2(math.e),
            list_len=list_len,
            pieces=table.shape[0] // turns,
        ),
        out_shape=jax.ShapeDtypeStruct((BLOCK, heads * width + BLOCK), jnp.bfloat16),
        in_specs=[smem] * 6 + [vmem] * (2 + len(q_parts)),
        out_specs=vmem,
        scratch_shapes=[
            pltpu.VMEM((BLOCK, heads * width), jnp.bfloat16),
            pltpu.VMEM((list_len + 1, BLOCK, BLOCK), jnp.float32),
            pltpu.VMEM((list_len + 1, BLOCK, BLOCK), jnp.float32),
            pltpu.VMEM((heads, BLOCK, BLOCK), jnp.float32),
        ],
        compiler_params=pltpu.CompilerParams(vmem_limit_bytes=VMEM_LIMIT),
        name="block_attention",
    )(jnp.full((1,), turn, jnp.int32), count, diag, klist, slist, table, keys, values, *q_parts)


def combine_kernel(*refs):
    outs, att_ref = refs[:-1], refs[-1]
    feats = att_ref.shape[1]
    width = outs[0].shape[1] - feats
    heads = feats // width
    lse = []
    for ref in outs:
        x = ref[:, feats:].astype(jnp.float32)
        lse.append(x + pltpu.roll(x, width - heads, 1) + pltpu.roll(x, width - 2 * heads, 1))
    top = lse[0]
    for x in lse[1:]:
        top = jnp.maximum(top, x)
    weight = [jnp.exp2(x - top) for x in lse]
    total = weight[0]
    for x in weight[1:]:
        total = total + x
    inverse = 1.0 / total
    weight = [x * inverse for x in weight]
    for h in range(heads):
        cols = slice(h * width, (h + 1) * width)
        mixed = outs[0][:, cols].astype(jnp.float32) * weight[0][:, h : h + 1]
        for ref, x in zip(outs[1:], weight[1:]):
            mixed = mixed + ref[:, cols].astype(jnp.float32) * x[:, h : h + 1]
        att_ref[:, cols] = mixed.astype(att_ref.dtype)


def combine(outs, feats):
    return pl.pallas_call(
        combine_kernel,
        out_shape=jax.ShapeDtypeStruct((outs[0].shape[0], feats), jnp.bfloat16),
        compiler_params=pltpu.CompilerParams(vmem_limit_bytes=VMEM_LIMIT),
        name="combine",
    )(*outs)


def project_kernel(order_ref, *refs, blocks, parts):
    *refs, away_ref, own_ref, rows_sc = refs
    att_refs, weight_refs = refs[:parts], refs[parts:]
    rows = blocks * BLOCK
    for i in range(parts):
        for k, ref in enumerate(att_refs):

            @pl.when(order_ref[i] == k)
            def _(i=i, ref=ref):
                rows_sc[i * BLOCK : (i + 1) * BLOCK, :] = ref[...]

    for m, ref in enumerate(weight_refs):
        out = jnp.dot(rows_sc[rows:, :], ref[...], preferred_element_type=jnp.float32)
        away_ref[m] = out.reshape(-1, rows, out.shape[1]).astype(away_ref.dtype)
        own_ref[m] = jnp.dot(rows_sc[:rows, :], ref[...], preferred_element_type=jnp.float32)


def project(order, blocks, atts, weights):
    rows, parts, plane = blocks * BLOCK, len(atts), len(weights)
    columns = weights[0].shape[1]
    vmem = pl.BlockSpec(memory_space=pltpu.VMEM)
    return pl.pallas_call(
        partial(project_kernel, blocks=blocks, parts=parts),
        out_shape=(
            jax.ShapeDtypeStruct((plane, parts // blocks - 1, rows, columns), jnp.bfloat16),
            jax.ShapeDtypeStruct((plane, rows, columns), jnp.float32),
        ),
        in_specs=[pl.BlockSpec(memory_space=pltpu.SMEM)] + [vmem] * (parts + plane),
        out_specs=(vmem, vmem),
        scratch_shapes=[pltpu.VMEM((parts * BLOCK, atts[0].shape[1]), jnp.bfloat16)],
        compiler_params=pltpu.CompilerParams(vmem_limit_bytes=VMEM_LIMIT),
        name="project",
    )(order, *atts, *weights)


def block_lists(vertical, slash, query_blocks, ids):
    local_blocks = ids.shape[0]
    offsets = query_blocks[:, None] - ids[None, :]
    vertical_hit = jnp.any(vertical[:, :, None] == ids[None, None, :], axis=1)
    slash_hit = jnp.any(slash[None, :, :, None] == offsets[:, None, None, :], axis=2)
    picked = (vertical_hit[None] | slash_hit) & (offsets > 0)[:, None, :]
    picked = picked.astype(jnp.int32)
    order = jnp.arange(local_blocks, dtype=jnp.int32)
    rank = jnp.sum(picked[:, :, None, :] * (order[None, :] < order[:, None]), axis=3)
    count = jnp.sum(picked, axis=2)
    list_len = -(-local_blocks // CHUNK) * CHUNK
    slot = jnp.arange(list_len, dtype=jnp.int32)
    wanted = jnp.where(slot[None, None, :] < count[:, :, None], slot[None, None, :], 0)
    match = picked[:, :, None, :] * (rank[:, :, None, :] == wanted[:, :, :, None])
    klist = jnp.sum(match * order, axis=3)
    slist = jnp.where(slot[None, None, :] < count[:, :, None], slot[None, None, :], list_len)
    own = query_blocks[:, None] == ids[None, :]
    diag = jnp.where(jnp.any(own, axis=1), jnp.sum(own * order, axis=1), -1).astype(jnp.int32)
    return count.reshape(-1), diag, klist.reshape(-1), slist.reshape(-1)


def plane_body(queries, cache_keys, cache_values, vertical_blocks, slash_offsets, out_weight):
    ctx_count = lax.axis_size("ctx")
    core_count = lax.axis_size("head")
    place = lax.axis_index("ctx")
    core = lax.axis_index("head")
    local_len, plane, width = cache_keys.shape
    lines = ctx_count // plane
    bits = plane.bit_length() - 1
    heads = vertical_blocks.shape[0] // plane
    feats = heads * width
    all_blocks = local_len // BLOCK * ctx_count

    def line_mask(k):
        return k << bits

    def plane_of(x):
        return x & (plane - 1)

    def line_of(x):
        return x >> bits

    mine, line = plane_of(place), line_of(place)

    def swap(x, mask):
        return lax.ppermute(x, "ctx", [(i, i ^ mask) for i in range(ctx_count)]) if mask else x

    q_own = jnp.concatenate(
        [
            swap(lax.dynamic_slice_in_dim(queries, (mine ^ m) * feats, feats, 1), m)
            for m in range(plane)
        ],
        axis=0,
    )

    def by_head(cache):
        heads_first = lax.optimization_barrier(jnp.transpose(cache, (1, 0, 2)))
        moved = [
            swap(lax.dynamic_index_in_dim(heads_first, mine ^ m, 0, keepdims=False), m)
            for m in range(plane)
        ]
        return jnp.concatenate(moved, axis=0)

    q_parts = []
    for k in range(lines):
        q_parts.append(swap(q_own, line_mask(k)))
    keys = by_head(cache_keys)
    values = by_head(cache_values)

    turns = line ^ jnp.arange(lines, dtype=jnp.int32)
    meta = block_lists(
        lax.dynamic_slice_in_dim(vertical_blocks, mine * heads, heads, 0),
        lax.dynamic_slice_in_dim(slash_offsets, mine * heads, heads, 0),
        all_blocks - lines + turns,
        jnp.concatenate(
            [
                (place ^ m) * (local_len // BLOCK)
                + jnp.arange(local_len // BLOCK, dtype=jnp.int32)
                for m in range(plane)
            ]
        ),
    )
    source = (turns[:, None] * plane + jnp.arange(plane, dtype=jnp.int32)[None, :]) ^ place
    table = (line_of(source) * plane + plane_of(source)).reshape(-1)
    share = lines // core_count
    steps = jnp.arange(core_count, dtype=jnp.int32)
    half = jnp.where(core + steps >= core_count, core + steps - core_count, core + steps)
    order = (half[:, None] * share + jnp.arange(share, dtype=jnp.int32)[None, :]).reshape(-1) ^ line

    keys, values, weight, table, order, meta, q_parts = lax.optimization_barrier(
        (keys, values, out_weight, table, order, meta, q_parts)
    )
    slabs = [lax.dynamic_slice_in_dim(weight, (mine ^ m) * feats, feats, 0) for m in range(plane)]
    weights = []
    for m in range(plane):
        weights.append(swap(slabs[m], m))

    outs = [None] * lines
    for k in reversed(range(lines)):
        o = block_attention(k, meta, table, q_parts, keys, values)
        if k:
            keys, o = lax.optimization_barrier((keys, o))
        outs[k] = swap(o, line_mask(k))
    att = combine(outs, feats)
    atts = [swap(att, line_mask(k)) for k in range(lines)]

    away, sums = project(order, share, atts, weights)
    for step in range(1, core_count):
        got = lax.ppermute(away[:, step - 1], "head", [(a, (a + step) % core_count) for a in range(core_count)])
        sums = sums + got.astype(jnp.float32)
    result = sums[0]
    for m in range(1, plane):
        result = result + swap(sums[m].astype(jnp.bfloat16), m).astype(jnp.float32)
    return result.astype(jnp.bfloat16)


def general_body(queries, cache_keys, cache_values, vertical_blocks, slash_offsets, out_weight):
    ctx_count = lax.axis_size("ctx")
    place = lax.axis_index("ctx")
    local_len, kv_local, width = cache_keys.shape
    heads = vertical_blocks.shape[0] // kv_local
    feats = heads * width
    q_whole = lax.all_gather(queries, "ctx", axis=0, tiled=True)
    q_blocks = q_whole.shape[0] // BLOCK
    local_blocks = local_len // BLOCK
    query_blocks = local_blocks * ctx_count - q_blocks + jnp.arange(q_blocks, dtype=jnp.int32)
    attention = []
    for g in range(kv_local):
        meta = block_lists(
            vertical_blocks[g * heads : (g + 1) * heads],
            slash_offsets[g * heads : (g + 1) * heads],
            query_blocks,
            place * local_blocks + jnp.arange(local_blocks, dtype=jnp.int32),
        )
        table = jnp.zeros((q_blocks,), jnp.int32)
        outs = []
        for b in range(q_blocks):
            q = q_whole[b * BLOCK : (b + 1) * BLOCK, g * feats : (g + 1) * feats]
            outs.append(block_attention(b, meta, table, [q], cache_keys[:, g, :], cache_values[:, g, :]))
        out = jnp.concatenate(outs, axis=0)
        lse = jnp.sum(out[:, feats : feats + 3 * heads].astype(jnp.float32).reshape(-1, 3, heads), axis=1)
        out = out[:, :feats].reshape(-1, heads, width)
        factor = jnp.exp2(lse - lax.pmax(lse, "ctx"))
        out, total = lax.psum((out.astype(jnp.float32) * factor[:, :, None], factor), "ctx")
        attention.append((out / total[:, :, None]).astype(jnp.bfloat16).reshape(-1, feats))
    return lax.psum_scatter(
        jnp.dot(jnp.concatenate(attention, axis=1), out_weight, preferred_element_type=jnp.float32),
        "head",
        scatter_dimension=0,
        tiled=True,
    ).astype(jnp.bfloat16)


def body(queries, cache_keys, cache_values, vertical_blocks, slash_offsets, out_weight):
    ctx_count = lax.axis_size("ctx")
    lines = queries.shape[0] * ctx_count // BLOCK
    plane, cores = cache_keys.shape[1], lax.axis_size("head")
    powers = all(n & (n - 1) == 0 for n in (plane, lines, cores))
    fits = powers and plane * lines == ctx_count and lines % cores == 0 and lines > 1
    chosen = plane_body if fits else general_body
    return chosen(queries, cache_keys, cache_values, vertical_blocks, slash_offsets, out_weight)


def solution(mesh):
    return jax.shard_map(
        body,
        mesh=mesh,
        in_specs=(
            P("ctx", "head"),
            P("ctx", "head", None),
            P("ctx", "head", None),
            P("head", None),
            P("head", None),
            P("head", "ctx"),
        ),
        out_specs=P("head", "ctx"),
        check_vma=False,
    )
```

```python
from functools import partial
import math

import jax
import jax.numpy as jnp
from jax import lax
from jax.experimental import pallas as pl
from jax.experimental.pallas import tpu as pltpu
from jax.sharding import PartitionSpec as P


BLOCK = 128
NEG_FILL = -1e30
CHUNK = 8
STEP = 2
VMEM_LIMIT = 20 << 20


def attention_kernel(
    turn_ref, count_ref, diag_ref, klist_ref, slist_ref, table_ref, k_ref, v_ref, *refs, scale2, list_len, pieces,
):
    *q_refs, o_ref, q_ref, even_sc, odd_sc, diag_sc, m_sc, total_sc, acc_sc = refs
    width = k_ref.shape[1]
    heads = q_ref.shape[1] // width
    turn = turn_ref[0]
    piece_rows = BLOCK // pieces
    for i in range(pieces):
        place = table_ref[turn * pieces + i]
        for j, ref in enumerate(q_refs):

            @pl.when(place // pieces == j)
            def _(i=i, j=j, ref=ref, place=place):
                start = pl.multiple_of((place - j * pieces) * piece_rows, piece_rows)
                q_ref[i * piece_rows : (i + 1) * piece_rows, :] = ref[pl.ds(start, piece_rows), :]

    diag = diag_ref[turn]
    bufs = (even_sc, odd_sc)

    def block_of(ref, index):
        return ref[pl.ds(pl.multiple_of(index * BLOCK, BLOCK), BLOCK), :]

    def scores_of(keys, h):
        q = q_ref[:, h * width : (h + 1) * width]
        s = lax.dot_general(q, keys, (((1,), (1,)), ((), ())), preferred_element_type=jnp.float32)
        return s * scale2

    for buf in bufs:
        buf[list_len] = jnp.full((BLOCK, BLOCK), NEG_FILL, jnp.float32)

    @pl.when(diag >= 0)
    def _():
        keys = block_of(k_ref, diag)
        causal = lax.broadcasted_iota(jnp.int32, (BLOCK, BLOCK), 1) <= lax.broadcasted_iota(
            jnp.int32, (BLOCK, BLOCK), 0
        )
        for h in range(heads):
            diag_sc[h] = jnp.where(causal, scores_of(keys, h), NEG_FILL)

    @pl.when(diag < 0)
    def _():
        diag_sc[...] = jnp.full(diag_sc.shape, NEG_FILL, jnp.float32)

    counts = [count_ref[turn * heads + h] for h in range(heads)]
    chunks = [(c + CHUNK - 1) // CHUNK for c in counts]

    def score_part(h, t, u, top):
        base = (turn * heads + h) * list_len + t * CHUNK + u
        keys = jnp.concatenate([block_of(k_ref, klist_ref[base + i]) for i in range(STEP)], axis=0)
        s = scores_of(keys, h)
        for i in range(STEP):
            part = s[:, i * BLOCK : (i + 1) * BLOCK]
            bufs[h % 2][t * CHUNK + u + i] = part
            top = jnp.maximum(top, part)
        return top

    def value_part(h, t, u, m, total, acc):
        base = (turn * heads + h) * list_len + t * CHUNK + u
        values = jnp.concatenate([block_of(v_ref, klist_ref[base + i]) for i in range(STEP)], axis=0)
        parts = [jnp.exp2(bufs[h % 2][slist_ref[base + i]] - m) for i in range(STEP)]
        for p in parts:
            total = total + p
        p = jnp.concatenate([p.astype(jnp.bfloat16) for p in parts], axis=1)
        return total, acc + jnp.dot(p, values, preferred_element_type=jnp.float32)

    top_start = jnp.full((BLOCK, BLOCK), NEG_FILL, jnp.float32)

    def first(t, top):
        for u in range(0, CHUNK, STEP):
            top = score_part(0, t, u, top)
        return top

    top = lax.fori_loop(0, chunks[0], first, top_start)
    zeros = jnp.zeros((BLOCK, BLOCK), jnp.float32)
    for h in range(heads):
        top = jnp.maximum(jnp.where(counts[h] > 0, top, NEG_FILL), diag_sc[h])
        m = jnp.max(top, axis=1, keepdims=True)
        if h + 1 < heads:

            def both(t, carry, h=h, m=m):
                top, total, acc = carry
                for u in range(0, CHUNK, STEP):
                    top = score_part(h + 1, t, u, top)
                    total, acc = value_part(h, t, u, m, total, acc)
                return top, total, acc

            top, total, acc = lax.fori_loop(
                0, jnp.maximum(chunks[h], chunks[h + 1]), both, (top_start, zeros, zeros)
            )
        else:

            def last(t, carry, h=h, m=m):
                for u in range(0, CHUNK, STEP):
                    carry = value_part(h, t, u, m, *carry)
                return carry

            total, acc = lax.fori_loop(0, chunks[h], last, (zeros, zeros))
        m_sc[h] = jnp.broadcast_to(m, (BLOCK, BLOCK))
        total_sc[h] = total
        acc_sc[h] = acc

    @pl.when(diag >= 0)
    def _():
        values = block_of(v_ref, diag)
        for h in range(heads):
            p = jnp.exp2(diag_sc[h] - m_sc[h])
            total_sc[h] += p
            acc_sc[h] += jnp.dot(p.astype(jnp.bfloat16), values, preferred_element_type=jnp.float32)

    lane = lax.broadcasted_iota(jnp.int32, (BLOCK, BLOCK), 1)
    lse = jnp.full((BLOCK, BLOCK), NEG_FILL, jnp.float32)
    for h in range(heads):
        total = jnp.sum(total_sc[h], axis=1, keepdims=True)
        seen = total > 0.0
        safe = jnp.where(seen, total, 1.0)
        o_ref[:, h * width : (h + 1) * width] = (acc_sc[h] * (1.0 / safe)).astype(o_ref.dtype)
        mine = (lane == h) | (lane == heads + h) | (lane == 2 * heads + h)
        lse = jnp.where(mine & seen, m_sc[h] + jnp.log2(safe), lse)
    high = lse.astype(jnp.bfloat16)
    rest = lse - high.astype(jnp.float32)
    middle = rest.astype(jnp.bfloat16)
    low = rest - middle.astype(jnp.float32)
    packed = jnp.where(lane < heads, high.astype(jnp.float32), jnp.where(lane < 2 * heads, middle.astype(jnp.float32), low))
    o_ref[:, heads * width :] = packed.astype(o_ref.dtype)


def block_attention(turn, meta, table, q_parts, keys, values):
    count, diag, klist, slist = meta
    turns = diag.shape[0]
    heads = count.shape[0] // turns
    width = keys.shape[1]
    list_len = klist.shape[0] // count.shape[0]
    smem = pl.BlockSpec(memory_space=pltpu.SMEM)
    vmem = pl.BlockSpec(memory_space=pltpu.VMEM)
    return pl.pallas_call(
        partial(
            attention_kernel,
            scale2=float(width) ** -0.5 * math.log2(math.e),
            list_len=list_len,
            pieces=table.shape[0] // turns,
        ),
        out_shape=jax.ShapeDtypeStruct((BLOCK, heads * width + BLOCK), jnp.bfloat16),
        in_specs=[smem] * 6 + [vmem] * (2 + len(q_parts)),
        out_specs=vmem,
        scratch_shapes=[
            pltpu.VMEM((BLOCK, heads * width), jnp.bfloat16),
            pltpu.VMEM((list_len + 1, BLOCK, BLOCK), jnp.float32),
            pltpu.VMEM((list_len + 1, BLOCK, BLOCK), jnp.float32),
        ]
        + [pltpu.VMEM((heads, BLOCK, BLOCK), jnp.float32)] * 4,
        compiler_params=pltpu.CompilerParams(vmem_limit_bytes=VMEM_LIMIT),
        name="block_attention",
    )(jnp.full((1,), turn, jnp.int32), count, diag, klist, slist, table, keys, values, *q_parts)


def combine_kernel(*refs):
    outs, att_ref = refs[:-1], refs[-1]
    feats = att_ref.shape[1]
    width = outs[0].shape[1] - feats
    heads = feats // width
    lse = []
    for ref in outs:
        x = ref[:, feats:].astype(jnp.float32)
        lse.append(x + pltpu.roll(x, width - heads, 1) + pltpu.roll(x, width - 2 * heads, 1))
    top = lse[0]
    for x in lse[1:]:
        top = jnp.maximum(top, x)
    weight = [jnp.exp2(x - top) for x in lse]
    total = weight[0]
    for x in weight[1:]:
        total = total + x
    inverse = 1.0 / total
    weight = [x * inverse for x in weight]
    for h in range(heads):
        cols = slice(h * width, (h + 1) * width)
        mixed = outs[0][:, cols].astype(jnp.float32) * weight[0][:, h : h + 1]
        for ref, x in zip(outs[1:], weight[1:]):
            mixed = mixed + ref[:, cols].astype(jnp.float32) * x[:, h : h + 1]
        att_ref[:, cols] = mixed.astype(att_ref.dtype)


def combine(outs, feats):
    return pl.pallas_call(
        combine_kernel,
        out_shape=jax.ShapeDtypeStruct((outs[0].shape[0], feats), jnp.bfloat16),
        compiler_params=pltpu.CompilerParams(vmem_limit_bytes=VMEM_LIMIT),
        name="combine",
    )(*outs)


def project_kernel(order_ref, *refs, blocks, parts):
    *refs, away_ref, own_ref, rows_sc = refs
    att_refs, weight_refs = refs[:parts], refs[parts:]
    rows = blocks * BLOCK
    for i in range(parts):
        for k, ref in enumerate(att_refs):

            @pl.when(order_ref[i] == k)
            def _(i=i, ref=ref):
                rows_sc[i * BLOCK : (i + 1) * BLOCK, :] = ref[...]

    for m, ref in enumerate(weight_refs):
        out = jnp.dot(rows_sc[rows:, :], ref[...], preferred_element_type=jnp.float32)
        away_ref[m] = out.reshape(-1, rows, out.shape[1]).astype(away_ref.dtype)
        own_ref[m] = jnp.dot(rows_sc[:rows, :], ref[...], preferred_element_type=jnp.float32)


def project(order, blocks, atts, weights):
    rows, parts, plane = blocks * BLOCK, len(atts), len(weights)
    columns = weights[0].shape[1]
    vmem = pl.BlockSpec(memory_space=pltpu.VMEM)
    return pl.pallas_call(
        partial(project_kernel, blocks=blocks, parts=parts),
        out_shape=(
            jax.ShapeDtypeStruct((plane, parts // blocks - 1, rows, columns), jnp.bfloat16),
            jax.ShapeDtypeStruct((plane, rows, columns), jnp.float32),
        ),
        in_specs=[pl.BlockSpec(memory_space=pltpu.SMEM)] + [vmem] * (parts + plane),
        out_specs=(vmem, vmem),
        scratch_shapes=[pltpu.VMEM((parts * BLOCK, atts[0].shape[1]), jnp.bfloat16)],
        compiler_params=pltpu.CompilerParams(vmem_limit_bytes=VMEM_LIMIT),
        name="project",
    )(order, *atts, *weights)


def block_lists(vertical, slash, query_blocks, ids):
    local_blocks = ids.shape[0]
    offsets = query_blocks[:, None] - ids[None, :]
    vertical_hit = jnp.any(vertical[:, :, None] == ids[None, None, :], axis=1)
    slash_hit = jnp.any(slash[None, :, :, None] == offsets[:, None, None, :], axis=2)
    picked = (vertical_hit[None] | slash_hit) & (offsets > 0)[:, None, :]
    picked = picked.astype(jnp.int32)
    order = jnp.arange(local_blocks, dtype=jnp.int32)
    rank = jnp.sum(picked[:, :, None, :] * (order[None, :] < order[:, None]), axis=3)
    count = jnp.sum(picked, axis=2)
    list_len = -(-local_blocks // CHUNK) * CHUNK
    slot = jnp.arange(list_len, dtype=jnp.int32)
    wanted = jnp.where(slot[None, None, :] < count[:, :, None], slot[None, None, :], 0)
    match = picked[:, :, None, :] * (rank[:, :, None, :] == wanted[:, :, :, None])
    klist = jnp.sum(match * order, axis=3)
    slist = jnp.where(slot[None, None, :] < count[:, :, None], slot[None, None, :], list_len)
    own = query_blocks[:, None] == ids[None, :]
    diag = jnp.where(jnp.any(own, axis=1), jnp.sum(own * order, axis=1), -1).astype(jnp.int32)
    return count.reshape(-1), diag, klist.reshape(-1), slist.reshape(-1)


def plane_body(queries, cache_keys, cache_values, vertical_blocks, slash_offsets, out_weight):
    ctx_count = lax.axis_size("ctx")
    core_count = lax.axis_size("head")
    place = lax.axis_index("ctx")
    core = lax.axis_index("head")
    local_len, plane, width = cache_keys.shape
    lines = ctx_count // plane
    bits = plane.bit_length() - 1
    heads = vertical_blocks.shape[0] // plane
    feats = heads * width
    all_blocks = local_len // BLOCK * ctx_count

    def line_mask(k):
        return k << bits

    def plane_of(x):
        return x & (plane - 1)

    def line_of(x):
        return x >> bits

    mine, line = plane_of(place), line_of(place)

    def swap(x, mask):
        return lax.ppermute(x, "ctx", [(i, i ^ mask) for i in range(ctx_count)]) if mask else x

    q_own = jnp.concatenate(
        [
            swap(lax.dynamic_slice_in_dim(queries, (mine ^ m) * feats, feats, 1), m)
            for m in range(plane)
        ],
        axis=0,
    )

    def by_head(cache):
        heads_first = lax.optimization_barrier(jnp.transpose(cache, (1, 0, 2)))
        moved = [
            swap(lax.dynamic_index_in_dim(heads_first, mine ^ m, 0, keepdims=False), m)
            for m in range(plane)
        ]
        return jnp.concatenate(moved, axis=0)

    q_parts = []
    for k in range(lines):
        q_parts.append(swap(q_own, line_mask(k)))
    keys = by_head(cache_keys)
    values = by_head(cache_values)

    turns = line ^ jnp.arange(lines, dtype=jnp.int32)
    meta = block_lists(
        lax.dynamic_slice_in_dim(vertical_blocks, mine * heads, heads, 0),
        lax.dynamic_slice_in_dim(slash_offsets, mine * heads, heads, 0),
        all_blocks - lines + turns,
        jnp.concatenate(
            [
                (place ^ m) * (local_len // BLOCK)
                + jnp.arange(local_len // BLOCK, dtype=jnp.int32)
                for m in range(plane)
            ]
        ),
    )
    source = (turns[:, None] * plane + jnp.arange(plane, dtype=jnp.int32)[None, :]) ^ place
    table = plane_of(source).reshape(-1)
    share = lines // core_count
    steps = jnp.arange(core_count, dtype=jnp.int32)
    half = jnp.where(core + steps >= core_count, core + steps - core_count, core + steps)
    order = (half[:, None] * share + jnp.arange(share, dtype=jnp.int32)[None, :]).reshape(-1) ^ line

    visits = ([2, 3, 1] + list(range(4, lines)) if lines >= 4 else list(range(1, lines))) + [0]
    keys, values, weight, table, order, meta, q_parts[visits[0]] = lax.optimization_barrier(
        (keys, values, out_weight, table, order, meta, q_parts[visits[0]])
    )
    slabs = [lax.dynamic_slice_in_dim(weight, (mine ^ m) * feats, feats, 0) for m in range(plane)]
    weights = []
    for m in range(plane):
        weights.append(swap(slabs[m], m))

    outs = [None] * lines
    for k in visits:
        o = block_attention(k, meta, table, [q_parts[k]], keys, values)
        if k:
            keys, o = lax.optimization_barrier((keys, o))
        outs[k] = swap(o, line_mask(k))
    att = combine(outs, feats)
    atts = [swap(att, line_mask(k)) for k in range(lines)]

    away, sums = project(order, share, atts, weights)
    for step in range(1, core_count):
        got = lax.ppermute(away[:, step - 1], "head", [(a, (a + step) % core_count) for a in range(core_count)])
        sums = sums + got.astype(jnp.float32)
    result = sums[0]
    for m in range(1, plane):
        result = result + swap(sums[m].astype(jnp.bfloat16), m).astype(jnp.float32)
    return result.astype(jnp.bfloat16)


def general_body(queries, cache_keys, cache_values, vertical_blocks, slash_offsets, out_weight):
    ctx_count = lax.axis_size("ctx")
    place = lax.axis_index("ctx")
    local_len, kv_local, width = cache_keys.shape
    heads = vertical_blocks.shape[0] // kv_local
    feats = heads * width
    q_whole = lax.all_gather(queries, "ctx", axis=0, tiled=True)
    q_blocks = q_whole.shape[0] // BLOCK
    local_blocks = local_len // BLOCK
    query_blocks = local_blocks * ctx_count - q_blocks + jnp.arange(q_blocks, dtype=jnp.int32)
    attention = []
    for g in range(kv_local):
        meta = block_lists(
            vertical_blocks[g * heads : (g + 1) * heads],
            slash_offsets[g * heads : (g + 1) * heads],
            query_blocks,
            place * local_blocks + jnp.arange(local_blocks, dtype=jnp.int32),
        )
        table = jnp.zeros((q_blocks,), jnp.int32)
        outs = []
        for b in range(q_blocks):
            q = q_whole[b * BLOCK : (b + 1) * BLOCK, g * feats : (g + 1) * feats]
            outs.append(block_attention(b, meta, table, [q], cache_keys[:, g, :], cache_values[:, g, :]))
        out = jnp.concatenate(outs, axis=0)
        lse = jnp.sum(out[:, feats : feats + 3 * heads].astype(jnp.float32).reshape(-1, 3, heads), axis=1)
        out = out[:, :feats].reshape(-1, heads, width)
        factor = jnp.exp2(lse - lax.pmax(lse, "ctx"))
        out, total = lax.psum((out.astype(jnp.float32) * factor[:, :, None], factor), "ctx")
        attention.append((out / total[:, :, None]).astype(jnp.bfloat16).reshape(-1, feats))
    return lax.psum_scatter(
        jnp.dot(jnp.concatenate(attention, axis=1), out_weight, preferred_element_type=jnp.float32),
        "head",
        scatter_dimension=0,
        tiled=True,
    ).astype(jnp.bfloat16)


def body(queries, cache_keys, cache_values, vertical_blocks, slash_offsets, out_weight):
    ctx_count = lax.axis_size("ctx")
    lines = queries.shape[0] * ctx_count // BLOCK
    plane, cores = cache_keys.shape[1], lax.axis_size("head")
    powers = all(n & (n - 1) == 0 for n in (plane, lines, cores))
    fits = powers and plane * lines == ctx_count and lines % cores == 0 and lines > 1
    chosen = plane_body if fits else general_body
    return chosen(queries, cache_keys, cache_values, vertical_blocks, slash_offsets, out_weight)


def solution(mesh):
    return jax.shard_map(
        body,
        mesh=mesh,
        in_specs=(
            P("ctx", "head"),
            P("ctx", "head", None),
            P("ctx", "head", None),
            P("head", None),
            P("head", None),
            P("head", "ctx"),
        ),
        out_specs=P("head", "ctx"),
        check_vma=False,
    )
```

```python
from functools import partial
import math

import jax
import jax.numpy as jnp
from jax import lax
from jax.experimental import pallas as pl
from jax.experimental.pallas import tpu as pltpu
from jax.sharding import PartitionSpec as P


BLOCK = 128
NEG_FILL = -1e30
CHUNK = 8
HALF = 4
STEP = 2
VMEM_LIMIT = 20 << 20


def attention_kernel(
    turn_ref, count_ref, diag_ref, klist_ref, slist_ref, table_ref, k_ref, v_ref, *refs, scale2, list_len, pieces,
):
    *q_refs, o_ref, q_ref, even_sc, odd_sc, diag_sc, m_sc, total_sc, acc_sc = refs
    width = k_ref.shape[1]
    heads = q_ref.shape[1] // width
    turn = turn_ref[0]
    piece_rows = BLOCK // pieces
    for i in range(pieces):
        place = table_ref[turn * pieces + i]
        for j, ref in enumerate(q_refs):

            @pl.when(place // pieces == j)
            def _(i=i, j=j, ref=ref, place=place):
                start = pl.multiple_of((place - j * pieces) * piece_rows, piece_rows)
                q_ref[i * piece_rows : (i + 1) * piece_rows, :] = ref[pl.ds(start, piece_rows), :]

    diag = diag_ref[turn]
    bufs = (even_sc, odd_sc)

    def block_of(ref, index):
        return ref[pl.ds(pl.multiple_of(index * BLOCK, BLOCK), BLOCK), :]

    def scores_of(keys, h):
        q = q_ref[:, h * width : (h + 1) * width]
        s = lax.dot_general(q, keys, (((1,), (1,)), ((), ())), preferred_element_type=jnp.float32)
        return s * scale2

    for buf in bufs:
        buf[list_len] = jnp.full((BLOCK, BLOCK), NEG_FILL, jnp.float32)

    @pl.when(diag >= 0)
    def _():
        keys = block_of(k_ref, diag)
        causal = lax.broadcasted_iota(jnp.int32, (BLOCK, BLOCK), 1) <= lax.broadcasted_iota(
            jnp.int32, (BLOCK, BLOCK), 0
        )
        for h in range(heads):
            diag_sc[h] = jnp.where(causal, scores_of(keys, h), NEG_FILL)

    @pl.when(diag < 0)
    def _():
        diag_sc[...] = jnp.full(diag_sc.shape, NEG_FILL, jnp.float32)

    counts = [count_ref[turn * heads + h] for h in range(heads)]
    chunks = [(c + HALF - 1) // HALF for c in counts]

    def score_part(h, slot, top):
        base = (turn * heads + h) * list_len + slot
        keys = jnp.concatenate([block_of(k_ref, klist_ref[base + i]) for i in range(STEP)], axis=0)
        s = scores_of(keys, h)
        for i in range(STEP):
            part = s[:, i * BLOCK : (i + 1) * BLOCK]
            bufs[h % 2][slot + i] = part
            top = jnp.maximum(top, part)
        return top

    def value_part(h, slot, m, total, acc):
        base = (turn * heads + h) * list_len + slot
        values = jnp.concatenate([block_of(v_ref, klist_ref[base + i]) for i in range(STEP)], axis=0)
        parts = [jnp.exp2(bufs[h % 2][slist_ref[base + i]] - m) for i in range(STEP)]
        for p in parts:
            total = total + p
        p = jnp.concatenate([p.astype(jnp.bfloat16) for p in parts], axis=1)
        return total, acc + jnp.dot(p, values, preferred_element_type=jnp.float32)

    top_start = jnp.full((BLOCK, BLOCK), NEG_FILL, jnp.float32)

    def walk(halves, visit, carry):
        wide = CHUNK // HALF

        def run(start, size, carry):
            for u in range(0, size, STEP):
                carry = visit(start + u, carry)
            return carry

        carry = lax.fori_loop(0, halves // wide, lambda t, c: run(t * CHUNK, CHUNK, c), carry)
        return lax.fori_loop(halves // wide * wide, halves, lambda t, c: run(t * HALF, HALF, c), carry)

    top = walk(chunks[0], lambda slot, top: score_part(0, slot, top), top_start)
    zeros = jnp.zeros((BLOCK, BLOCK), jnp.float32)
    for h in range(heads):
        top = jnp.maximum(jnp.where(counts[h] > 0, top, NEG_FILL), diag_sc[h])
        m = jnp.max(top, axis=1, keepdims=True)
        if h + 1 < heads:

            def both(slot, carry, h=h, m=m):
                top, total, acc = carry
                top = score_part(h + 1, slot, top)
                return (top,) + value_part(h, slot, m, total, acc)

            top, total, acc = walk(jnp.maximum(chunks[h], chunks[h + 1]), both, (top_start, zeros, zeros))
        else:

            def last(slot, carry, h=h, m=m):
                return value_part(h, slot, m, *carry)

            total, acc = walk(chunks[h], last, (zeros, zeros))
        m_sc[h] = jnp.broadcast_to(m, (BLOCK, BLOCK))
        total_sc[h] = total
        acc_sc[h] = acc

    @pl.when(diag >= 0)
    def _():
        values = block_of(v_ref, diag)
        for h in range(heads):
            p = jnp.exp2(diag_sc[h] - m_sc[h])
            total_sc[h] += p
            acc_sc[h] += jnp.dot(p.astype(jnp.bfloat16), values, preferred_element_type=jnp.float32)

    lane = lax.broadcasted_iota(jnp.int32, (BLOCK, BLOCK), 1)
    lse = jnp.full((BLOCK, BLOCK), NEG_FILL, jnp.float32)
    for h in range(heads):
        total = jnp.sum(total_sc[h], axis=1, keepdims=True)
        seen = total > 0.0
        safe = jnp.where(seen, total, 1.0)
        o_ref[:, h * width : (h + 1) * width] = (acc_sc[h] * (1.0 / safe)).astype(o_ref.dtype)
        mine = (lane == h) | (lane == heads + h) | (lane == 2 * heads + h)
        lse = jnp.where(mine & seen, m_sc[h] + jnp.log2(safe), lse)
    high = lse.astype(jnp.bfloat16)
    rest = lse - high.astype(jnp.float32)
    middle = rest.astype(jnp.bfloat16)
    low = rest - middle.astype(jnp.float32)
    packed = jnp.where(lane < heads, high.astype(jnp.float32), jnp.where(lane < 2 * heads, middle.astype(jnp.float32), low))
    o_ref[:, heads * width :] = packed.astype(o_ref.dtype)


def block_attention(turn, meta, table, q_parts, keys, values):
    count, diag, klist, slist = meta
    turns = diag.shape[0]
    heads = count.shape[0] // turns
    width = keys.shape[1]
    list_len = klist.shape[0] // count.shape[0]
    smem = pl.BlockSpec(memory_space=pltpu.SMEM)
    vmem = pl.BlockSpec(memory_space=pltpu.VMEM)
    return pl.pallas_call(
        partial(
            attention_kernel,
            scale2=float(width) ** -0.5 * math.log2(math.e),
            list_len=list_len,
            pieces=table.shape[0] // turns,
        ),
        out_shape=jax.ShapeDtypeStruct((BLOCK, heads * width + BLOCK), jnp.bfloat16),
        in_specs=[smem] * 6 + [vmem] * (2 + len(q_parts)),
        out_specs=vmem,
        scratch_shapes=[
            pltpu.VMEM((BLOCK, heads * width), jnp.bfloat16),
            pltpu.VMEM((list_len + 1, BLOCK, BLOCK), jnp.float32),
            pltpu.VMEM((list_len + 1, BLOCK, BLOCK), jnp.float32),
        ]
        + [pltpu.VMEM((heads, BLOCK, BLOCK), jnp.float32)] * 4,
        compiler_params=pltpu.CompilerParams(vmem_limit_bytes=VMEM_LIMIT),
        name="block_attention",
    )(jnp.full((1,), turn, jnp.int32), count, diag, klist, slist, table, keys, values, *q_parts)


def combine_kernel(*refs):
    outs, att_ref = refs[:-1], refs[-1]
    feats = att_ref.shape[1]
    width = outs[0].shape[1] - feats
    heads = feats // width
    lse = []
    for ref in outs:
        x = ref[:, feats:].astype(jnp.float32)
        lse.append(x + pltpu.roll(x, width - heads, 1) + pltpu.roll(x, width - 2 * heads, 1))
    top = lse[0]
    for x in lse[1:]:
        top = jnp.maximum(top, x)
    weight = [jnp.exp2(x - top) for x in lse]
    total = weight[0]
    for x in weight[1:]:
        total = total + x
    inverse = 1.0 / total
    weight = [x * inverse for x in weight]
    for h in range(heads):
        cols = slice(h * width, (h + 1) * width)
        mixed = outs[0][:, cols].astype(jnp.float32) * weight[0][:, h : h + 1]
        for ref, x in zip(outs[1:], weight[1:]):
            mixed = mixed + ref[:, cols].astype(jnp.float32) * x[:, h : h + 1]
        att_ref[:, cols] = mixed.astype(att_ref.dtype)


def combine(outs, feats):
    return pl.pallas_call(
        combine_kernel,
        out_shape=jax.ShapeDtypeStruct((outs[0].shape[0], feats), jnp.bfloat16),
        compiler_params=pltpu.CompilerParams(vmem_limit_bytes=VMEM_LIMIT),
        name="combine",
    )(*outs)


def project_kernel(order_ref, *refs, blocks, parts):
    *refs, away_ref, own_ref, rows_sc = refs
    att_refs, weight_refs = refs[:parts], refs[parts:]
    rows = blocks * BLOCK
    for i in range(parts):
        for k, ref in enumerate(att_refs):

            @pl.when(order_ref[i] == k)
            def _(i=i, ref=ref):
                rows_sc[i * BLOCK : (i + 1) * BLOCK, :] = ref[...]

    for m, ref in enumerate(weight_refs):
        out = jnp.dot(rows_sc[rows:, :], ref[...], preferred_element_type=jnp.float32)
        away_ref[m] = out.reshape(-1, rows, out.shape[1]).astype(away_ref.dtype)
        own_ref[m] = jnp.dot(rows_sc[:rows, :], ref[...], preferred_element_type=jnp.float32)


def project(order, blocks, atts, weights):
    rows, parts, plane = blocks * BLOCK, len(atts), len(weights)
    columns = weights[0].shape[1]
    vmem = pl.BlockSpec(memory_space=pltpu.VMEM)
    return pl.pallas_call(
        partial(project_kernel, blocks=blocks, parts=parts),
        out_shape=(
            jax.ShapeDtypeStruct((plane, parts // blocks - 1, rows, columns), jnp.bfloat16),
            jax.ShapeDtypeStruct((plane, rows, columns), jnp.float32),
        ),
        in_specs=[pl.BlockSpec(memory_space=pltpu.SMEM)] + [vmem] * (parts + plane),
        out_specs=(vmem, vmem),
        scratch_shapes=[pltpu.VMEM((parts * BLOCK, atts[0].shape[1]), jnp.bfloat16)],
        compiler_params=pltpu.CompilerParams(vmem_limit_bytes=VMEM_LIMIT),
        name="project",
    )(order, *atts, *weights)


def block_lists(vertical, slash, query_blocks, ids):
    local_blocks = ids.shape[0]
    offsets = query_blocks[:, None] - ids[None, :]
    vertical_hit = jnp.any(vertical[:, :, None] == ids[None, None, :], axis=1)
    slash_hit = jnp.any(slash[None, :, :, None] == offsets[:, None, None, :], axis=2)
    picked = (vertical_hit[None] | slash_hit) & (offsets > 0)[:, None, :]
    picked = picked.astype(jnp.int32)
    order = jnp.arange(local_blocks, dtype=jnp.int32)
    rank = jnp.sum(picked[:, :, None, :] * (order[None, :] < order[:, None]), axis=3)
    count = jnp.sum(picked, axis=2)
    list_len = -(-local_blocks // CHUNK) * CHUNK
    slot = jnp.arange(list_len, dtype=jnp.int32)
    wanted = jnp.where(slot[None, None, :] < count[:, :, None], slot[None, None, :], 0)
    match = picked[:, :, None, :] * (rank[:, :, None, :] == wanted[:, :, :, None])
    klist = jnp.sum(match * order, axis=3)
    slist = jnp.where(slot[None, None, :] < count[:, :, None], slot[None, None, :], list_len)
    own = query_blocks[:, None] == ids[None, :]
    diag = jnp.where(jnp.any(own, axis=1), jnp.sum(own * order, axis=1), -1).astype(jnp.int32)
    return count.reshape(-1), diag, klist.reshape(-1), slist.reshape(-1)


def plane_body(queries, cache_keys, cache_values, vertical_blocks, slash_offsets, out_weight):
    ctx_count = lax.axis_size("ctx")
    core_count = lax.axis_size("head")
    place = lax.axis_index("ctx")
    core = lax.axis_index("head")
    local_len, plane, width = cache_keys.shape
    lines = ctx_count // plane
    bits = plane.bit_length() - 1
    heads = vertical_blocks.shape[0] // plane
    feats = heads * width
    all_blocks = local_len // BLOCK * ctx_count

    def line_mask(k):
        return k << bits

    def plane_of(x):
        return x & (plane - 1)

    def line_of(x):
        return x >> bits

    mine, line = plane_of(place), line_of(place)

    def swap(x, mask):
        return lax.ppermute(x, "ctx", [(i, i ^ mask) for i in range(ctx_count)]) if mask else x

    q_own = jnp.concatenate(
        [swap(lax.dynamic_slice_in_dim(queries, (mine ^ m) * feats, feats, 1), m) for m in range(plane)],
        axis=0,
    )

    def by_head(cache):
        heads_first = lax.optimization_barrier(jnp.transpose(cache, (1, 0, 2)))
        moved = [swap(lax.dynamic_index_in_dim(heads_first, mine ^ m, 0, keepdims=False), m) for m in range(plane)]
        return jnp.concatenate(moved, axis=0)

    q_parts = []
    for k in range(lines):
        q_parts.append(swap(q_own, line_mask(k)))
    keys = by_head(cache_keys)
    values = by_head(cache_values)

    turns = line ^ jnp.arange(lines, dtype=jnp.int32)
    meta = block_lists(
        lax.dynamic_slice_in_dim(vertical_blocks, mine * heads, heads, 0),
        lax.dynamic_slice_in_dim(slash_offsets, mine * heads, heads, 0),
        all_blocks - lines + turns,
        jnp.concatenate(
            [(place ^ m) * (local_len // BLOCK) + jnp.arange(local_len // BLOCK, dtype=jnp.int32) for m in range(plane)]
        ),
    )
    source = (turns[:, None] * plane + jnp.arange(plane, dtype=jnp.int32)[None, :]) ^ place
    table = plane_of(source).reshape(-1)
    share = lines // core_count
    steps = jnp.arange(core_count, dtype=jnp.int32)
    half = jnp.where(core + steps >= core_count, core + steps - core_count, core + steps)
    order = (half[:, None] * share + jnp.arange(share, dtype=jnp.int32)[None, :]).reshape(-1) ^ line

    visits = ([2, 1, 3] + list(range(4, lines)) if lines >= 4 else list(range(1, lines))) + [0]
    keys, values, weight, table, order, meta, q_parts[visits[0]] = lax.optimization_barrier(
        (keys, values, out_weight, table, order, meta, q_parts[visits[0]])
    )
    slabs = [lax.dynamic_slice_in_dim(weight, (mine ^ m) * feats, feats, 0) for m in range(plane)]
    weights = []
    for m in range(plane):
        weights.append(swap(slabs[m], m))

    outs = [None] * lines
    for k in visits:
        o = block_attention(k, meta, table, [q_parts[k]], keys, values)
        if k:
            keys, o = lax.optimization_barrier((keys, o))
        outs[k] = swap(o, line_mask(k))
    att = combine(outs, feats)
    atts = [swap(att, line_mask(k)) for k in range(lines)]

    away, sums = project(order, share, atts, weights)
    for step in range(1, core_count):
        got = lax.ppermute(away[:, step - 1], "head", [(a, (a + step) % core_count) for a in range(core_count)])
        sums = sums + got.astype(jnp.float32)
    result = sums[0]
    for m in range(1, plane):
        result = result + swap(sums[m].astype(jnp.bfloat16), m).astype(jnp.float32)
    return result.astype(jnp.bfloat16)


def general_body(queries, cache_keys, cache_values, vertical_blocks, slash_offsets, out_weight):
    ctx_count = lax.axis_size("ctx")
    place = lax.axis_index("ctx")
    local_len, kv_local, width = cache_keys.shape
    heads = vertical_blocks.shape[0] // kv_local
    feats = heads * width
    q_whole = lax.all_gather(queries, "ctx", axis=0, tiled=True)
    q_blocks = q_whole.shape[0] // BLOCK
    local_blocks = local_len // BLOCK
    query_blocks = local_blocks * ctx_count - q_blocks + jnp.arange(q_blocks, dtype=jnp.int32)
    attention = []
    for g in range(kv_local):
        meta = block_lists(
            vertical_blocks[g * heads : (g + 1) * heads],
            slash_offsets[g * heads : (g + 1) * heads],
            query_blocks,
            place * local_blocks + jnp.arange(local_blocks, dtype=jnp.int32),
        )
        table = jnp.zeros((q_blocks,), jnp.int32)
        outs = []
        for b in range(q_blocks):
            q = q_whole[b * BLOCK : (b + 1) * BLOCK, g * feats : (g + 1) * feats]
            outs.append(block_attention(b, meta, table, [q], cache_keys[:, g, :], cache_values[:, g, :]))
        out = jnp.concatenate(outs, axis=0)
        lse = jnp.sum(out[:, feats : feats + 3 * heads].astype(jnp.float32).reshape(-1, 3, heads), axis=1)
        out = out[:, :feats].reshape(-1, heads, width)
        factor = jnp.exp2(lse - lax.pmax(lse, "ctx"))
        out, total = lax.psum((out.astype(jnp.float32) * factor[:, :, None], factor), "ctx")
        attention.append((out / total[:, :, None]).astype(jnp.bfloat16).reshape(-1, feats))
    return lax.psum_scatter(
        jnp.dot(jnp.concatenate(attention, axis=1), out_weight, preferred_element_type=jnp.float32),
        "head",
        scatter_dimension=0,
        tiled=True,
    ).astype(jnp.bfloat16)


def body(queries, cache_keys, cache_values, vertical_blocks, slash_offsets, out_weight):
    ctx_count = lax.axis_size("ctx")
    lines = queries.shape[0] * ctx_count // BLOCK
    plane, cores = cache_keys.shape[1], lax.axis_size("head")
    powers = all(n & (n - 1) == 0 for n in (plane, lines, cores))
    fits = powers and plane * lines == ctx_count and lines % cores == 0 and lines > 1
    chosen = plane_body if fits else general_body
    return chosen(queries, cache_keys, cache_values, vertical_blocks, slash_offsets, out_weight)


def solution(mesh):
    return jax.shard_map(
        body,
        mesh=mesh,
        in_specs=(
            P("ctx", "head"),
            P("ctx", "head", None),
            P("ctx", "head", None),
            P("head", None),
            P("head", None),
            P("head", "ctx"),
        ),
        out_specs=P("head", "ctx"),
        check_vma=False,
    )
```
